32 devices in a mesh: pb: 8 (over y, x, core), wa: 4 (over z).
Axes of the slice: x: 2, y: 2, z: 4, core: 2. Of those that a mesh axis runs over, the one named last changes fastest.
Arguments:
- acts: bfloat16 [2048, 28672], P('pb', 'wa'), may hold values from -6 to 6
- grads: bfloat16 [2048, 8192], P('pb', 'wa'), may hold values from -6 to 6
- query_in: bfloat16 [28672, 4096], P('wa', 'pb'), may hold values from -0.03125 to 0.03125
- query_out: bfloat16 [8192, 4096], P('wa', 'pb'), may hold values from -0.01171875 to 0.01171875
- lengths: int32 [128], replicated, may hold values from 1 to 128, 2048 in all
Outputs:
- seq_scores: float32 [128, 128], P('pb', 'wa')
The draws below stay inside these ranges and needn't reach their ends.
Inputs may be any that keep to these rules, and one draw needn't show every extreme that they name: The lengths sum to 2048 and the longest is exactly 128.
All inputs are finite; a program needn't handle non-finite values.
Results may differ from the reference program's by a relative error of at most 0.0003.
Values may be sent and summed in bfloat16 or wider, within the bound.
A program may use at most 64 MiB of HBM per device.

```python
import math
import jax
import jax.numpy as jnp
import numpy as np
from jax import lax

D_IN = 28672
D_OUT = 8192
QUERIES = 128
RANK = 32
TOK_DEV = 256
TOKENS = 2048
NSEQ = 128
SEQ_MOST = 128
WINDOW = 4
N_PB = 8


def with_spikes(array, stream_key, source, target, shards_of, factor):
    owner, partner = [(jnp.arange(array.shape[axis_at]) // (array.shape[axis_at] // shards_of)).reshape([-1 if axis == axis_at else 1 for axis in range(array.ndim)]) for axis_at in (source, target)]
    chosen = jax.random.permutation(stream_key, shards_of)[partner]
    strong = (owner == chosen) | (owner == (partner + shards_of // 2) % shards_of)
    return jnp.where(strong, factor * array, array)


def levels(key, extent, split, least, largest):
    def one(axis_at, parts):
        draws = jax.random.uniform(jax.random.fold_in(jax.random.fold_in(key, 6), axis_at), (parts,), jnp.float32, least / len(split), largest / len(split))
        return jnp.repeat(jnp.exp(draws), extent[axis_at] // parts).reshape((-1,) + (1,) * (len(extent) - axis_at - 1))

    loudness = one(*split[0])
    for cut in split[1:]:
        loudness = loudness * one(*cut)
    return loudness


def profile(amount, total, reach, slope):
    loads = [(1 << 20) // math.isqrt(grade ** slope) + 1 for grade in range(2, amount + 1)]
    surplus, holding = total - reach - (amount - 1), [1] * (amount - 1)
    while surplus > 0:
        movable = [i for i in range(amount - 1) if holding[i] < reach]
        mass, remaining = sum([loads[i] for i in movable]), surplus
        for i in movable:
            extra = min(reach - holding[i], max(1, remaining * loads[i] // mass), surplus)
            holding[i] = holding[i] + extra
            surplus = surplus - extra
    return np.array([reach] + holding)


def ragged_sizes(key, number_of, total, reach, skew):
    if number_of == 2:
        one = jax.random.randint(key, (), max(1, total - reach), min(reach, total - 1) + 1)
        return jnp.stack([one, total - one])
    tallies = jnp.asarray(profile(number_of, total, reach, skew), jnp.int32)
    twos = (number_of - 1) // 2
    source_of, sink = tallies[1:1 + 2 * twos:2], tallies[2:2 + 2 * twos:2]
    slack = jnp.minimum(source_of - 1, reach - sink)
    shifted = jax.random.randint(jax.random.fold_in(key, 1), (twos,), 0, 1 << 20) % (slack + 1)
    tallies = tallies.at[1:1 + 2 * twos:2].set(source_of - shifted).at[2:2 + 2 * twos:2].set(sink + shifted)
    return tallies[jax.random.permutation(jax.random.fold_in(key, 2), number_of)]


def centred(rng, shape, width, limit, pieces=(), kind=jnp.bfloat16):
    result = jax.random.normal(rng, shape, jnp.float32) * width
    if len(pieces) > 0:
        result = levels(rng, shape, pieces, -0.22, 0.18) * result
    return jnp.clip(result, min=-limit, max=limit).astype(kind)


def heavy_noise(key, shape, deviation, most, shards, heavy, kind=jnp.bfloat16):
    values = deviation * jax.random.normal(key, shape, jnp.float32)
    if shards:
        values = values * levels(key, shape, shards, -0.22, 0.18)
    return jnp.clip(with_spikes(values, jax.random.fold_in(key, 3), *heavy), -most, most).astype(kind)


def setup_inputs(seed: int = 0) -> dict:
    splits = jax.random.split(jax.random.key(seed), 6)
    acts = heavy_noise(splits[0], (TOKENS, D_IN), 1.0, 6.0, ((0, 8), (1, 4)), (1, 0, 8, 2.0))
    grads = centred(splits[1], (TOKENS, D_OUT), 1.0, 6.0, ((0, 8), (1, 4)))
    query_in = centred(splits[2], (D_IN, QUERIES * RANK), D_IN ** -0.5, 0.03125, ((0, 4), (1, 8)))
    query_out = centred(splits[3], (D_OUT, QUERIES * RANK), (D_OUT * RANK) ** -0.5, 0.01171875, ((0, 4), (1, 8)))
    lengths = ragged_sizes(splits[4], NSEQ, TOKENS, SEQ_MOST, 2).astype(jnp.int32)
    return dict(acts=acts, grads=grads, query_in=query_in, query_out=query_out, lengths=lengths)


def reference(acts, grads, query_in, query_out, lengths):
    proj_in = jnp.dot(acts, query_in, preferred_element_type=jnp.float32)
    proj_out = jnp.dot(grads, query_out, preferred_element_type=jnp.float32)
    token_score = jnp.sum((proj_in * proj_out).reshape(TOKENS, QUERIES, RANK), axis=2)
    blocks = (lax.iota(jnp.int32, TOKENS) // TOK_DEV).astype(jnp.int32)
    qgroups = (lax.iota(jnp.int32, QUERIES) // (QUERIES // N_PB)).astype(jnp.int32)
    offset = (qgroups[None, :] - blocks[:, None] + N_PB) % N_PB
    kept = jnp.where(offset < WINDOW, token_score, jnp.zeros_like(token_score))
    ends = jnp.cumsum(lengths).astype(jnp.int32)
    starts = (ends - lengths).astype(jnp.int32)
    spots = lax.iota(jnp.int32, TOKENS)
    inside = (spots[:, None] >= starts[None, :]) & (spots[:, None] < ends[None, :])
    table = inside.astype(token_score.dtype)
    seq_total = jnp.dot(kept.T, table, precision=lax.Precision.HIGHEST)
    return seq_total / lengths.astype(token_score.dtype)[None, :]
```

```python
import functools

import jax
import jax.numpy as jnp
from jax import lax
from jax.experimental import pallas as pl
from jax.experimental.pallas import tpu as pltpu
from jax.sharding import PartitionSpec as P

RANK = 32
MESH = pl.DeviceIdType.MESH
HIGHEST = lax.Precision.HIGHEST


def kernel(
    groups, widths, chunks,
    acts_ref, grads_ref, qin_ref, qout_ref, lengths_ref,
    out_ref,
    own_in, own_out, fac_in, fac_out, tok_in, tok_out,
    part, got, prods, table, tot, tot_got,
    load_sem, own_send, fwd_send, relay_send, tok_recv,
    part_send, part_recv, tot_send, tot_recv,
):
    window = groups // 2
    chips = groups // 2
    half = window // 2
    tok = acts_ref.shape[0]
    rows = tok // chunks
    share = rows // widths
    cols = qin_ref.shape[1]
    nseq = lengths_ref.shape[1]
    slots = window - 1

    g = lax.axis_index("pb")
    w = lax.axis_index("wa")
    core = lax.rem(g, 2)
    chip = g // 2
    even_core = core == 0
    odd_chip = lax.rem(chip, 2) == 1

    def device(chip_at, core_at):
        return lax.rem(chip_at + chips, chips) * 2 + core_at

    partner = chip * 2 + 1 - core

    loads = [
        pltpu.make_async_copy(acts_ref, own_in, load_sem.at[0]),
        pltpu.make_async_copy(qin_ref, fac_in, load_sem.at[1]),
        pltpu.make_async_copy(grads_ref, own_out, load_sem.at[2]),
        pltpu.make_async_copy(qout_ref, fac_out, load_sem.at[3]),
    ]
    for load in loads:
        load.start()

    barrier = pltpu.get_barrier_semaphore()
    for step in range(1, groups):
        pl.semaphore_signal(
            barrier, inc=1, device_id={"pb": lax.rem(g + step, groups)}, device_id_type=MESH
        )
    for step in range(1, widths):
        pl.semaphore_signal(
            barrier, inc=1, device_id={"wa": lax.rem(w + step, widths)}, device_id_type=MESH
        )
    pl.semaphore_wait(barrier, groups + widths - 2)

    sources = (acts_ref, grads_ref)
    tokens = (tok_in, tok_out)

    def send_own(kind, chunk, slot, target):
        span = pl.ds(chunk * rows, rows)
        for half_at in range(2):
            pltpu.make_async_remote_copy(
                src_ref=sources[half_at].at[span],
                dst_ref=tokens[half_at].at[slot - 1, span],
                send_sem=own_send.at[half_at, kind],
                recv_sem=tok_recv.at[half_at, slot - 1, chunk],
                device_id={"pb": target},
                device_id_type=MESH,
            ).start()

    def own_done(kind):
        for half_at in range(2):
            pltpu.make_async_copy(
                sources[half_at], sources[half_at], own_send.at[half_at, kind]
            ).wait()

    def send_on(chunk, slot, sem, slot_there, target):
        span = pl.ds(chunk * rows, rows)
        for half_at in range(2):
            pltpu.make_async_remote_copy(
                src_ref=tokens[half_at].at[slot - 1, span],
                dst_ref=tokens[half_at].at[slot_there - 1, span],
                send_sem=sem(half_at),
                recv_sem=tok_recv.at[half_at, slot_there - 1, chunk],
                device_id={"pb": target},
                device_id_type=MESH,
            ).start()

    def direct_next(j):
        if j == 1:
            return jnp.logical_or(even_core, jnp.logical_not(odd_chip))
        return None

    for chunk in range(chunks):
        @pl.when(jnp.logical_not(even_core))
        def _():
            send_own(0, chunk, window - 1, device(chip + half, 0))

        for j in range(1, half):
            condition = direct_next(j)
            if condition is None:
                send_own(j, chunk, 2 * j, device(chip + j, core))
            else:
                @pl.when(condition)
                def _():
                    send_own(j, chunk, 2 * j, device(chip + j, core))

        @pl.when(even_core)
        def _():
            send_own(0, chunk, 1, partner)

    def wait_for(ref, sem):
        pltpu.make_async_copy(ref, ref, sem).wait()

    def split(depth):
        piece = depth
        while piece > 1024 and piece % 256 == 0:
            piece //= 2
        return piece

    def project(left, fac, place, column):
        depth = fac.shape[0]
        piece = split(depth)

        def body(i, total):
            span = pl.ds(pl.multiple_of(i * piece, piece), piece)
            return total + jnp.dot(
                left(span), fac[span, :], preferred_element_type=jnp.float32
            )

        part[place, :, column:column + cols] = lax.fori_loop(
            0, depth // piece, body, jnp.zeros((rows, cols), jnp.float32)
        )

    def exchange(place):
        for step in range(1, widths):
            peer = lax.rem(w + step, widths)
            pltpu.make_async_remote_copy(
                src_ref=part.at[place, pl.ds(pl.multiple_of(peer * share, share), share)],
                dst_ref=got.at[place, step - 1],
                send_sem=part_send.at[place],
                recv_sem=part_recv.at[place],
                device_id={"wa": peer},
                device_id_type=MESH,
            ).start()

    lengths_float = lengths_ref[...].astype(jnp.float32)

    def settle(place, slot, chunk):
        wait_for(got.at[place], part_recv.at[place])
        total = part[place, pl.ds(pl.multiple_of(w * share, share), share), :]
        for step in range(widths - 1):
            total = total + got[place, step]
        into = pl.ds(pl.multiple_of(place * share, share), share)
        prods[into, :] = total[:, :cols] * total[:, cols:]
        anchor = lax.rem(g - slot + groups, groups)
        first = anchor * tok + chunk * rows + w * share
        spots = first + lax.broadcasted_iota(jnp.int32, (share, nseq), 0)
        table[into, :] = spots

    def own_chunk(chunk, carry):
        span = pl.ds(pl.multiple_of(chunk * rows, rows), rows)
        project(lambda at: own_in[span, at], fac_in, chunk, 0)
        project(lambda at: own_out[span, at], fac_out, chunk, cols)
        exchange(chunk)
        return carry

    for load in loads:
        load.wait()
    lax.fori_loop(0, chunks, own_chunk, 0)

    even_order = [window - 1]
    odd_order = [1]
    for j in range(1, half):
        even_order += [2 * j, 2 * j - 1]
        odd_order += [2 * j, 2 * j + 1]

    def slot_of(p):
        return jnp.where(even_core, even_order[p], odd_order[p])

    relays = jnp.logical_and(even_core, lax.rem(chip - half + chips, 2) == 1)

    def arrived(chunk, carry):
        span = pl.ds(pl.multiple_of(chunk * rows, rows), rows)
        for p in range(slots):
            slot = slot_of(p)
            for half_at in range(2):
                wait_for(
                    tokens[half_at].at[slot - 1, span], tok_recv.at[half_at, slot - 1, chunk]
                )
            if p == 0 and half > 1:
                @pl.when(relays)
                def _():
                    send_on(
                        chunk, slot, lambda at: relay_send.at[at], 2,
                        device(chip - half + 1, 1),
                    )
            if p % 2 == 1:
                there = jnp.where(even_core, p + 2, p)
                send_on(
                    chunk, slot, lambda at: fwd_send.at[at, p // 2], there, partner
                )
            place = chunks + chunk * slots + p
            project(lambda at: tok_in[slot - 1, span, at], fac_in, place, 0)
            project(lambda at: tok_out[slot - 1, span, at], fac_out, place, cols)
            exchange(place)
            if p == 0:
                settle(chunk, 0, chunk)
            else:
                @pl.when(chunk > 0)
                def _():
                    settle(place - slots - 1, slot_of(p - 1), chunk - 1)

        @pl.when(chunk > 0)
        def _():
            settle(chunks + chunk * slots - 1, slot_of(slots - 1), chunk - 1)

        return carry

    lax.fori_loop(0, chunks, arrived, 0)
    for p in range(slots):
        settle(chunks + (chunks - 1) * slots + p, slot_of(p), chunks - 1)

    upto = (
        lax.broadcasted_iota(jnp.int32, (nseq, nseq), 0)
        <= lax.broadcasted_iota(jnp.int32, (nseq, nseq), 1)
    ).astype(jnp.float32)
    wide = jnp.broadcast_to(lengths_float, (8, nseq))
    ends = jnp.dot(
        wide, upto, precision=HIGHEST, preferred_element_type=jnp.float32
    )[0:1, :].astype(jnp.int32)
    starts = ends - lengths_ref[...]
    spots = table[...]
    inside = ((spots >= starts) & (spots < ends)).astype(jnp.float32)
    local_q = cols // RANK
    chooses = (
        lax.broadcasted_iota(jnp.int32, (local_q, cols), 1) // RANK
        == lax.broadcasted_iota(jnp.int32, (local_q, cols), 0)
    ).astype(jnp.float32)
    scores = lax.dot_general(
        chooses, prods[...], (((1,), (1,)), ((), ())),
        precision=HIGHEST, preferred_element_type=jnp.float32,
    )
    tot[...] = jnp.dot(
        scores, inside, precision=HIGHEST, preferred_element_type=jnp.float32
    )
    for step in range(1, widths):
        pltpu.make_async_remote_copy(
            src_ref=tot,
            dst_ref=tot_got.at[step - 1],
            send_sem=tot_send.at[step - 1],
            recv_sem=tot_recv.at[step - 1],
            device_id={"wa": lax.rem(w + step, widths)},
            device_id_type=MESH,
        ).start()

    own_done_needed = [(0, None)]
    own_done(0)
    for j in range(1, half):
        condition = direct_next(j)
        if condition is None:
            own_done(j)
        else:
            @pl.when(condition)
            def _():
                own_done(j)
        for half_at in range(2):
            wait_for(tokens[half_at].at[0], fwd_send.at[half_at, j - 1])
    if half > 1:
        @pl.when(relays)
        def _():
            for half_at in range(2):
                wait_for(tokens[half_at].at[0], relay_send.at[half_at])

    def part_done(place, carry):
        wait_for(got.at[place], part_send.at[place])
        return carry

    lax.fori_loop(0, chunks * window, part_done, 0)

    total = tot[...]
    for step in range(widths - 1):
        wait_for(tot_got.at[step], tot_recv.at[step])
        total = total + tot_got[step]
    for step in range(widths - 1):
        wait_for(tot, tot_send.at[step])
    out_ref[...] = total / lengths_float


def shards(groups, widths, acts, grads, query_in, query_out, lengths):
    tok, d_in = acts.shape
    d_out = grads.shape[1]
    cols = query_in.shape[1]
    nseq = lengths.shape[0]
    window = groups // 2
    half = window // 2
    chunks = max(1, min(4, tok // (8 * widths)))
    rows = tok // chunks
    share = rows // widths
    slots = window - 1
    places = chunks * window
    local_q = cols // RANK
    bf16, f32 = jnp.bfloat16, jnp.float32
    dma = pltpu.SemaphoreType.DMA
    vmem = pltpu.VMEM
    whole = pl.BlockSpec(memory_space=pl.ANY)
    full = pl.pallas_call(
        functools.partial(kernel, groups, widths, chunks),
        out_shape=jax.ShapeDtypeStruct((local_q, nseq), f32),
        in_specs=[whole] * 4 + [pl.BlockSpec(memory_space=pltpu.VMEM)],
        out_specs=pl.BlockSpec(memory_space=pltpu.VMEM),
        scratch_shapes=[
            vmem((tok, d_in), bf16),
            vmem((tok, d_out), bf16),
            vmem((d_in, cols), bf16),
            vmem((d_out, cols), bf16),
            vmem((slots, tok, d_in), bf16),
            vmem((slots, tok, d_out), bf16),
            vmem((places, rows, 2 * cols), f32),
            vmem((places, widths - 1, share, 2 * cols), f32),
            vmem((places * share, cols), f32),
            vmem((places * share, nseq), jnp.int32),
            vmem((local_q, nseq), f32),
            vmem((widths - 1, local_q, nseq), f32),
            dma((4,)),
            dma((2, max(half, 1))),
            dma((2, max(half - 1, 1))),
            dma((2,)),
            dma((2, slots, chunks)),
            dma((places,)),
            dma((places,)),
            dma((widths - 1,)),
            dma((widths - 1,)),
        ],
        compiler_params=pltpu.CompilerParams(
            collective_id=0, has_side_effects=True, vmem_limit_bytes=60 << 20
        ),
    )(acts, grads, query_in, query_out, lengths.reshape(1, nseq))
    seqs = nseq // widths
    return lax.dynamic_slice_in_dim(full, lax.axis_index("wa") * seqs, seqs, 1)


def solution(mesh):
    return jax.shard_map(
        functools.partial(shards, mesh.shape["pb"], mesh.shape["wa"]),
        mesh=mesh,
        in_specs=(P("pb", "wa"), P("pb", "wa"), P("wa", "pb"), P("wa", "pb"), P()),
        out_specs=P("pb", "wa"),
        check_vma=False,
    )
```

```python
import functools

import jax
import jax.numpy as jnp
from jax import lax
from jax.experimental import pallas as pl
from jax.experimental.pallas import tpu as pltpu
from jax.sharding import PartitionSpec as P

RANK = 32
MESH = pl.DeviceIdType.MESH
HIGHEST = lax.Precision.HIGHEST


def kernel(
    groups, widths, chunks,
    acts_ref, grads_ref, qin_ref, qout_ref, lengths_ref,
    out_ref,
    own_in, own_out, fac_in, fac_out, tok_in, tok_out,
    part, got, prods, table, tot, tot_got,
    load_sem, own_send, fwd_send, relay_send, tok_recv,
    part_send, part_recv, tot_send, tot_recv,
):
    window = groups // 2
    chips = groups // 2
    half = window // 2
    tok = acts_ref.shape[0]
    rows = tok // chunks
    cols = qin_ref.shape[1]
    nseq = lengths_ref.shape[1]
    slots = window - 1
    lag = 3

    g = lax.axis_index("pb")
    w = lax.axis_index("wa")
    core = lax.rem(g, 2)
    chip = g // 2
    even_core = core == 0
    odd_chip = lax.rem(chip, 2) == 1

    def device(chip_at, core_at):
        return lax.rem(chip_at + chips, chips) * 2 + core_at

    partner = chip * 2 + 1 - core

    loads = [
        pltpu.make_async_copy(acts_ref, own_in, load_sem.at[0]),
        pltpu.make_async_copy(qin_ref, fac_in, load_sem.at[1]),
        pltpu.make_async_copy(grads_ref, own_out, load_sem.at[2]),
        pltpu.make_async_copy(qout_ref, fac_out, load_sem.at[3]),
    ]
    for load in loads:
        load.start()

    barrier = pltpu.get_barrier_semaphore()
    for step in range(1, groups):
        pl.semaphore_signal(
            barrier, inc=1, device_id={"pb": lax.rem(g + step, groups)}, device_id_type=MESH
        )
    for step in range(1, widths):
        pl.semaphore_signal(
            barrier, inc=1, device_id={"wa": lax.rem(w + step, widths)}, device_id_type=MESH
        )
    pl.semaphore_wait(barrier, groups + widths - 2)

    sources = (acts_ref, grads_ref)
    tokens = (tok_in, tok_out)

    def send_own(kind, chunk, slot, target):
        span = pl.ds(pl.multiple_of(chunk * rows, rows), rows)
        for half_at in range(2):
            pltpu.make_async_remote_copy(
                src_ref=sources[half_at].at[span],
                dst_ref=tokens[half_at].at[slot - 1, span],
                send_sem=own_send.at[half_at, kind],
                recv_sem=tok_recv.at[half_at, slot - 1, chunk],
                device_id={"pb": target},
                device_id_type=MESH,
            ).start()

    def own_done(kind):
        for half_at in range(2):
            pltpu.make_async_copy(
                sources[half_at], sources[half_at], own_send.at[half_at, kind]
            ).wait()

    def send_on(chunk, slot, sem, slot_there, target):
        span = pl.ds(pl.multiple_of(chunk * rows, rows), rows)
        for half_at in range(2):
            pltpu.make_async_remote_copy(
                src_ref=tokens[half_at].at[slot - 1, span],
                dst_ref=tokens[half_at].at[slot_there - 1, span],
                send_sem=sem(half_at),
                recv_sem=tok_recv.at[half_at, slot_there - 1, chunk],
                device_id={"pb": target},
                device_id_type=MESH,
            ).start()

    def direct_next(j):
        if j == 1:
            return jnp.logical_or(even_core, jnp.logical_not(odd_chip))
        return None

    for chunk in range(chunks):
        @pl.when(jnp.logical_not(even_core))
        def _():
            send_own(0, chunk, window - 1, device(chip + half, 0))

        for j in range(1, half):
            condition = direct_next(j)
            if condition is None:
                send_own(j, chunk, 2 * j, device(chip + j, core))
            else:
                @pl.when(condition)
                def _():
                    send_own(j, chunk, 2 * j, device(chip + j, core))

        @pl.when(even_core)
        def _():
            send_own(0, chunk, 1, partner)

    def wait_for(ref, sem):
        pltpu.make_async_copy(ref, ref, sem).wait()

    def split(depth):
        piece = depth
        while piece > 1024 and piece % 256 == 0:
            piece //= 2
        return piece

    def project(left, fac, at, size, column):
        depth = fac.shape[0]
        piece = split(depth)

        def body(i, total):
            span = pl.ds(pl.multiple_of(i * piece, piece), piece)
            return total + jnp.dot(
                left(span), fac[span, :], preferred_element_type=jnp.float32
            )

        part[at:at + size, column:column + cols] = lax.fori_loop(
            0, depth // piece, body, jnp.zeros((size, cols), jnp.float32)
        )

    def exchange(place):
        at, size = steps[place][:2]
        share = size // widths
        for step in range(1, widths):
            peer = lax.rem(w + step, widths)
            pltpu.make_async_remote_copy(
                src_ref=part.at[pl.ds(pl.multiple_of(at + peer * share, share), share)],
                dst_ref=got.at[step - 1, pl.ds(at // widths, share)],
                send_sem=part_send.at[place],
                recv_sem=part_recv.at[place],
                device_id={"wa": peer},
                device_id_type=MESH,
            ).start()

    def parcel(place):
        at, size = steps[place][:2]
        return got.at[:, pl.ds(at // widths, size // widths)]

    lengths_float = lengths_ref[...].astype(jnp.float32)

    def settle(place):
        at, size, slot, row = steps[place]
        share = size // widths
        wait_for(parcel(place), part_recv.at[place])
        total = part[pl.ds(pl.multiple_of(at + w * share, share), share), :]
        into = slice(at // widths, at // widths + share)
        for step in range(widths - 1):
            total = total + got[step, into, :]
        prods[into, :] = total[:, :cols] * total[:, cols:]
        anchor = lax.rem(g - slot + groups, groups)
        first = anchor * tok + row + w * share
        table[into, :] = first + lax.broadcasted_iota(jnp.int32, (share, nseq), 0)

    span_of = range(chunks)
    direct = [2 * j for j in range(1, half)]
    even_chip_even = [(k, c) for k in direct for c in span_of]
    for c in span_of:
        even_chip_even += [(window - 1, c)] + [(k - 1, c) for k in direct]
    even_chip_odd = [(1, c) for c in span_of]
    even_chip_odd += [(k + 1, c) for k in direct for c in span_of]
    even_chip_odd += [(k, c) for k in direct for c in span_of]

    def woven(first, other):
        order = []
        for c in span_of:
            order += [(first, at) for at in (2 * c, 2 * c + 1) if at < chunks]
            for k in direct:
                order += [(k, c), (k + other, c)]
        return order

    odd_chip_even = woven(window - 1, -1)
    odd_chip_odd = woven(1, 1)

    def role(step, field):
        return jnp.where(
            odd_chip,
            jnp.where(even_core, odd_chip_even[step][field], odd_chip_odd[step][field]),
            jnp.where(even_core, even_chip_even[step][field], even_chip_odd[step][field]),
        )

    steps = []
    own_rows = tok // 2
    for i in range(2):
        steps.append((i * own_rows, own_rows, 0, i * own_rows))
    for i in range(slots * chunks):
        steps.append((tok + i * rows, rows, role(i, 0), role(i, 1) * rows))

    for load in loads:
        load.wait()
    for i in range(2):
        span = pl.ds(i * own_rows, own_rows)
        project(lambda at: own_in[span, at], fac_in, i * own_rows, own_rows, 0)
        project(lambda at: own_out[span, at], fac_out, i * own_rows, own_rows, cols)
        exchange(i)

    relays = jnp.logical_and(even_core, lax.rem(chip - half + chips, 2) == 1)

    for i in range(slots * chunks):
        slot, chunk = role(i, 0), role(i, 1)
        span = pl.ds(pl.multiple_of(chunk * rows, rows), rows)
        for half_at in range(2):
            wait_for(
                tokens[half_at].at[slot - 1, span], tok_recv.at[half_at, slot - 1, chunk]
            )
        if half > 1:
            @pl.when(jnp.logical_and(relays, slot == window - 1))
            def _():
                send_on(
                    chunk, slot, lambda at: relay_send.at[at], 2,
                    device(chip - half + 1, 1),
                )

            @pl.when(lax.rem(slot, 2) == 0)
            def _():
                there = jnp.where(even_core, slot + 1, slot - 1)
                send_on(
                    chunk, slot, lambda at: fwd_send.at[at, slot // 2 - 1], there, partner
                )
        at, size = steps[2 + i][:2]
        project(lambda to: tok_in[slot - 1, span, to], fac_in, at, size, 0)
        project(lambda to: tok_out[slot - 1, span, to], fac_out, at, size, cols)
        exchange(2 + i)
        if i >= lag:
            settle(2 + i - lag)
        if i == lag:
            settle(0)
            settle(1)

    for i in range(max(0, slots * chunks - lag), slots * chunks):
        settle(2 + i)
    if slots * chunks <= lag:
        settle(0)
        settle(1)

    upto = (
        lax.broadcasted_iota(jnp.int32, (nseq, nseq), 0)
        <= lax.broadcasted_iota(jnp.int32, (nseq, nseq), 1)
    ).astype(jnp.float32)
    wide = jnp.broadcast_to(lengths_float, (8, nseq))
    ends = jnp.dot(
        wide, upto, precision=HIGHEST, preferred_element_type=jnp.float32
    )[0:1, :].astype(jnp.int32)
    starts = ends - lengths_ref[...]
    spots = table[...]
    inside = ((spots >= starts) & (spots < ends)).astype(jnp.float32)
    local_q = cols // RANK
    chooses = (
        lax.broadcasted_iota(jnp.int32, (local_q, cols), 1) // RANK
        == lax.broadcasted_iota(jnp.int32, (local_q, cols), 0)
    ).astype(jnp.float32)
    scores = lax.dot_general(
        chooses, prods[...], (((1,), (1,)), ((), ())),
        precision=HIGHEST, preferred_element_type=jnp.float32,
    )
    tot[...] = jnp.dot(
        scores, inside, precision=HIGHEST, preferred_element_type=jnp.float32
    )
    for step in range(1, widths):
        pltpu.make_async_remote_copy(
            src_ref=tot,
            dst_ref=tot_got.at[step - 1],
            send_sem=tot_send.at[step - 1],
            recv_sem=tot_recv.at[step - 1],
            device_id={"wa": lax.rem(w + step, widths)},
            device_id_type=MESH,
        ).start()

    own_done(0)
    for j in range(1, half):
        condition = direct_next(j)
        if condition is None:
            own_done(j)
        else:
            @pl.when(condition)
            def _():
                own_done(j)
        for half_at in range(2):
            wait_for(tokens[half_at].at[0], fwd_send.at[half_at, j - 1])
    if half > 1:
        @pl.when(relays)
        def _():
            for half_at in range(2):
                wait_for(tokens[half_at].at[0], relay_send.at[half_at])

    for place in range(len(steps)):
        wait_for(parcel(place), part_send.at[place])

    total = tot[...]
    for step in range(widths - 1):
        wait_for(tot_got.at[step], tot_recv.at[step])
        total = total + tot_got[step]
    for step in range(widths - 1):
        wait_for(tot, tot_send.at[step])
    out_ref[...] = total / lengths_float


def shards(groups, widths, acts, grads, query_in, query_out, lengths):
    tok, d_in = acts.shape
    d_out = grads.shape[1]
    cols = query_in.shape[1]
    nseq = lengths.shape[0]
    window = groups // 2
    half = window // 2
    chunks = max(1, min(4, tok // (8 * widths)))
    slots = window - 1
    places = 2 + chunks * slots
    local_q = cols // RANK
    bf16, f32 = jnp.bfloat16, jnp.float32
    dma = pltpu.SemaphoreType.DMA
    vmem = pltpu.VMEM
    whole = pl.BlockSpec(memory_space=pl.ANY)
    full = pl.pallas_call(
        functools.partial(kernel, groups, widths, chunks),
        out_shape=jax.ShapeDtypeStruct((local_q, nseq), f32),
        in_specs=[whole] * 4 + [pl.BlockSpec(memory_space=pltpu.VMEM)],
        out_specs=pl.BlockSpec(memory_space=pltpu.VMEM),
        scratch_shapes=[
            vmem((tok, d_in), bf16),
            vmem((tok, d_out), bf16),
            vmem((d_in, cols), bf16),
            vmem((d_out, cols), bf16),
            vmem((slots, tok, d_in), bf16),
            vmem((slots, tok, d_out), bf16),
            vmem((window * tok, 2 * cols), f32),
            vmem((widths - 1, window * tok // widths, 2 * cols), f32),
            vmem((window * tok // widths, cols), f32),
            vmem((window * tok // widths, nseq), jnp.int32),
            vmem((local_q, nseq), f32),
            vmem((widths - 1, local_q, nseq), f32),
            dma((4,)),
            dma((2, max(half, 1))),
            dma((2, max(half - 1, 1))),
            dma((2,)),
            dma((2, slots, chunks)),
            dma((places,)),
            dma((places,)),
            dma((widths - 1,)),
            dma((widths - 1,)),
        ],
        compiler_params=pltpu.CompilerParams(
            collective_id=0, has_side_effects=True, vmem_limit_bytes=60 << 20
        ),
    )(acts, grads, query_in, query_out, lengths.reshape(1, nseq))
    seqs = nseq // widths
    return lax.dynamic_slice_in_dim(full, lax.axis_index("wa") * seqs, seqs, 1)


def solution(mesh):
    return jax.shard_map(
        functools.partial(shards, mesh.shape["pb"], mesh.shape["wa"]),
        mesh=mesh,
        in_specs=(P("pb", "wa"), P("pb", "wa"), P("wa", "pb"), P("wa", "pb"), P()),
        out_specs=P("pb", "wa"),
        check_vma=False,
    )
```
